32 devices in a mesh: mod: 4 (over y, x), blk: 8 (over z, core).
Axes of the slice: x: 2, y: 2, z: 4, core: 2. Of those that a mesh axis runs over, the one named last changes fastest.
Arguments:
- intensity: bfloat16 [32768, 1024], P('mod', 'blk'), may hold values from 0.1 to 810
- pixel_bin: int32 [32768], replicated, may hold values from 0 to 199, as said below
Outputs:
- two_time: float32 [200, 32, 32], P('mod', 'blk')
The draws below stay inside these ranges and needn't reach their ends.
Inputs may be any that keep to these rules, and one draw needn't show every extreme that they name: `pixel_bin`: owner o holds the bins o * 50 to (o + 1) * 50 - 1. Of the 8192 pixels of one module group (an aligned block of entries), at most 4096 lie in the bins of one owner, and in every draw some owner receives exactly 4096 from every module group. Every bin holds at least one pixel.
All inputs are finite; a program needn't handle non-finite values.
Results may differ from the reference program's by a relative error of at most 0.0007.
Values may be sent and summed in bfloat16 or wider, within the bound.
No kernel may reach another device: no remote copies, remote signals or barrier semaphores. Data moves between devices by JAX's collectives and lax.ppermute only.
A program may use at most 128 MiB of HBM per device.

```python
import math
import jax
import jax.numpy as jnp
from jax import lax

NBINS = 200
F = 128
TBIN = 4
PIX_MOD = 8192
POOL = 32
PIX = 32768
FRAMES = 1024
TT = 32
N_BLK = 8


def draw_intensity(key, part):
    key_gain = jax.random.fold_in(key, 11)
    key_frame = jax.random.fold_in(key, 12)
    key_speckle = jax.random.fold_in(key, 13)
    key_first = jax.random.fold_in(key, 14)
    key_second = jax.random.fold_in(key, 15)
    key_mixing = jax.random.fold_in(key, 16)
    mixing = jax.random.uniform(key_mixing, (TT,), jnp.float32, 0.0, 1.0)
    mix_frames = jnp.repeat(mixing, POOL)[None, :]
    gains = jnp.exp(jax.random.uniform(key_gain, (PIX, 1), jnp.float32, 0.0, math.log(10.0)))
    frame_scale = jnp.exp(jax.random.uniform(key_frame, (1, FRAMES), jnp.float32, 0.0, math.log(10.0)))
    first_pattern = jnp.minimum(-jnp.log(jax.random.uniform(key_first, (PIX, 1), jnp.float32, 1e-06, 1.0)), 4.0)
    second_pattern = jnp.minimum(-jnp.log(jax.random.uniform(key_second, (PIX, 1), jnp.float32, 1e-06, 1.0)), 4.0)
    fresh = jnp.minimum(-jnp.log(jax.random.uniform(key_speckle, (PIX, FRAMES), jnp.float32, 1e-06, 1.0)), 4.0)
    speckle = 0.1 + 0.6 * (mix_frames * first_pattern + (1.0 - mix_frames) * second_pattern) + 0.4 * fresh
    return (gains * frame_scale * speckle).astype(jnp.bfloat16)


def draw_pixel_bin(key, part):
    module_count = PIX // PIX_MOD
    bins_owned = NBINS // module_count
    slot_size = PIX_MOD // 2
    remaining = PIX_MOD - slot_size
    heavy = jax.random.randint(jax.random.fold_in(key, 21), (), 0, module_count)
    weights = jax.random.randint(jax.random.fold_in(key, 22), (module_count, module_count), 6, 9)
    owners = jnp.arange(module_count, dtype=jnp.int32)
    is_heavy = owners[None, :] == heavy
    weights = jnp.where(is_heavy, 0, weights)
    shares = remaining * weights // jnp.sum(weights, axis=1, keepdims=True)
    leftover = remaining - jnp.sum(shares, axis=1, keepdims=True)
    shares = shares + jnp.where(owners[None, :] == (heavy + 1) % module_count, leftover, 0)
    shares = jnp.where(is_heavy, slot_size, shares)
    bounds = jnp.cumsum(shares, axis=1)
    position = jnp.arange(PIX_MOD, dtype=jnp.int32)
    owner_of = jnp.sum((position[None, :, None] >= bounds[:, None, :]).astype(jnp.int32), axis=2)
    starts_in_module = bounds - shares
    earlier = jnp.cumsum(shares, axis=0) - shares
    offset = jnp.take_along_axis(earlier - starts_in_module, owner_of, axis=1)
    index_in_owner = position[None, :] + offset
    random_bins = jax.random.randint(jax.random.fold_in(key, 23), (module_count, PIX_MOD), 0, bins_owned)
    local_bin = jnp.where(index_in_owner < bins_owned, index_in_owner, random_bins)
    ordered = owner_of * bins_owned + local_bin
    module_keys = jax.random.split(jax.random.fold_in(key, 24), module_count)
    orders = jax.vmap(lambda module_key: jax.random.permutation(module_key, PIX_MOD))(module_keys)
    shuffled = jnp.take_along_axis(ordered, orders, axis=1)
    return shuffled.reshape(PIX).astype(jnp.int32)


def setup_inputs(seed: int = 0) -> dict:
    splits = jax.random.split(jax.random.key(seed), 3)
    return {
        "intensity": draw_intensity(jax.random.fold_in(splits[2], 71), 0),
        "pixel_bin": draw_pixel_bin(jax.random.fold_in(splits[2], 71), 0),
    }


def reference(intensity, pixel_bin):
    counts = jax.ops.segment_sum(jnp.ones((PIX,), jnp.float32), pixel_bin, num_segments=NBINS)

    def one_block(first_frame):
        frame_slab = lax.dynamic_slice_in_dim(intensity, first_frame, F, 1).astype(jnp.float32)
        totals = jax.ops.segment_sum(frame_slab, pixel_bin, num_segments=NBINS)
        bin_mean = totals / counts[:, None]
        ratios = frame_slab / bin_mean[pixel_bin]
        return ratios.reshape(PIX, TBIN, POOL).sum(axis=2) / POOL

    block_starts = (jnp.arange(N_BLK) * F).astype(jnp.int32)
    per_block = lax.map(one_block, block_starts)
    pooled = jnp.transpose(per_block, (1, 0, 2)).reshape(PIX, TT).astype(jnp.bfloat16)
    widened = pooled.astype(jnp.float32)

    def one_row(column_vals):
        products = widened * column_vals[:, None]
        return jax.ops.segment_sum(products, pixel_bin, num_segments=NBINS)

    gram_rows = lax.map(one_row, widened.T)
    return jnp.transpose(gram_rows, (1, 0, 2)) / counts[:, None, None]
```

```python
import functools

import jax
import jax.numpy as jnp
from jax import lax
from jax.experimental import pallas as pl
from jax.experimental.pallas import tpu as pltpu
from jax.sharding import PartitionSpec as P

NBINS = 200
TBIN = 4
F32 = jnp.float32
BF16 = jnp.bfloat16
NT = (((1,), (1,)), ((), ()))
TN = (((0,), (0,)), ((), ()))


def round_up(value, multiple):
    return (value + multiple - 1) // multiple * multiple


def onehot_rows(index_row, rows):
    row_ids = lax.broadcasted_iota(jnp.int32, (rows, index_row.shape[1]), 0)
    return jnp.where(row_ids == index_row, 1.0, 0.0).astype(BF16)


def split_hi_lo(value):
    hi = value.astype(BF16)
    lo = (value - hi.astype(F32)).astype(BF16)
    return hi, lo


def totals_kernel(bins_ref, intensity_ref, out_ref, *, chunk):
    rows, _ = out_ref.shape
    acc = jnp.zeros(out_ref.shape, F32)
    for start in range(0, bins_ref.shape[1], chunk):
        onehot = onehot_rows(bins_ref[:, start : start + chunk], rows)
        acc += jnp.dot(onehot, intensity_ref[start : start + chunk, :], preferred_element_type=F32)
    out_ref[...] = acc


def prepare_kernel(bins_ref, intensity_ref, counts_ref, flipped_ref, *, chunk):
    rows, lanes = counts_ref.shape
    frames = intensity_ref.shape[1]
    eye = (
        lax.broadcasted_iota(jnp.int32, (frames, frames), 0)
        == lax.broadcasted_iota(jnp.int32, (frames, frames), 1)
    )
    eye = jnp.where(eye, 1.0, 0.0).astype(BF16)
    for start in range(0, intensity_ref.shape[0], chunk):
        block = intensity_ref[start : start + chunk, :]
        flipped = lax.dot_general(eye, block, NT, preferred_element_type=F32)
        flipped_ref[:, start : start + chunk] = flipped.astype(BF16)
    row_ids = lax.broadcasted_iota(jnp.int32, (rows, lanes), 0)

    def step(k, acc):
        piece = bins_ref[:, pl.ds(pl.multiple_of(k * 8 * lanes, 8 * lanes), 8 * lanes)]
        for s in range(8):
            acc += jnp.where(row_ids == piece[:, s * lanes : (s + 1) * lanes], 1.0, 0.0)
        return acc

    acc = lax.fori_loop(0, bins_ref.shape[1] // (8 * lanes), step, jnp.zeros((rows, lanes), F32))
    counts_ref[...] = jnp.broadcast_to(jnp.sum(acc, axis=1, keepdims=True), (rows, lanes))


def pool_kernel(bins_ref, counts_ref, flipped_ref, own_ref, *rest, chunk):
    *other_refs, out_ref = rest
    rows, frames = own_ref.shape
    totals = own_ref[...]
    for other in other_refs:
        totals += other[...]
    pool = frames // out_ref.shape[0]
    counts = counts_ref[...]
    weights = counts / (jnp.where(counts > 0.0, totals, 1.0) * float(pool))
    hi, lo = split_hi_lo(weights)
    both = jnp.concatenate([hi, lo], axis=1)
    for start in range(0, bins_ref.shape[1], chunk):
        onehot = onehot_rows(bins_ref[:, start : start + chunk], rows)
        spread = lax.dot_general(both, onehot, TN, preferred_element_type=F32)
        spread = spread[:frames, :] + spread[frames:, :]
        ratios = flipped_ref[:, start : start + chunk].astype(F32) * spread
        pooled = [
            jnp.sum(ratios[i * pool : (i + 1) * pool, :], axis=0, keepdims=True)
            for i in range(out_ref.shape[0])
        ]
        out_ref[:, start : start + chunk] = jnp.concatenate(pooled, axis=0).astype(BF16)


def gram_kernel(index_ref, own_ref, all_ref, out_ref, *, chunk):
    rows = out_ref.shape[0]
    tbin = own_ref.shape[0]
    cols = all_ref.shape[0]
    width = tbin * cols
    acc = jnp.zeros((rows, 2 * width), F32)
    for start in range(0, index_ref.shape[1], chunk):
        onehot = onehot_rows(index_ref[:, start : start + chunk], rows)
        own = own_ref[:, start : start + chunk].astype(F32)
        every = all_ref[:, start : start + chunk].astype(F32)
        his, los = [], []
        for i in range(tbin):
            hi, lo = split_hi_lo(own[i : i + 1, :] * every)
            his.append(hi)
            los.append(lo)
        products = jnp.concatenate(his + los, axis=0)
        acc += lax.dot_general(onehot, products, NT, preferred_element_type=F32)
    out_ref[...] = acc[:, :width] + acc[:, width:]


def call(kernel, out_shape, *args, flops, limit=48 << 20):
    vmem = pl.BlockSpec(memory_space=pltpu.VMEM)
    shapes = out_shape if isinstance(out_shape, tuple) else (out_shape,)
    moved = sum(a.size * a.dtype.itemsize for a in args)
    moved += sum(s.size * s.dtype.itemsize for s in shapes)
    return pl.pallas_call(
        kernel,
        out_shape=out_shape,
        in_specs=[vmem] * len(args),
        out_specs=(vmem,) * len(shapes) if isinstance(out_shape, tuple) else vmem,
        compiler_params=pltpu.CompilerParams(vmem_limit_bytes=limit),
        cost_estimate=pl.CostEstimate(flops=flops, bytes_accessed=moved, transcendentals=0),
    )(*args)


def swap(value, axis, distance):
    size = lax.axis_size(axis)
    return lax.ppermute(value, axis, [(i, i ^ distance) for i in range(size)])


def gather_blocks(pooled):
    n_blk = lax.axis_size("blk")
    if n_blk > 8 or n_blk % 2:
        return lax.all_gather(pooled, "blk", axis=0, tiled=True)
    k = lax.axis_index("blk")
    same_core = [pooled] + [swap(pooled, "blk", 2 * s) for s in range(1, n_blk // 2)]
    mine = jnp.stack(same_core)
    sibling = swap(mine, "blk", 1)
    pairs = jnp.stack([mine, sibling], axis=1)
    flat = pairs.reshape((n_blk,) + pooled.shape)
    order = jnp.arange(n_blk, dtype=jnp.int32) ^ k
    return flat[order].reshape(n_blk * pooled.shape[0], pooled.shape[1])


def body(intensity, pixel_bin):
    n_mod = lax.axis_size("mod")
    n_blk = lax.axis_size("blk")
    module = lax.axis_index("mod")
    pixels, frames = intensity.shape
    bins_owned = NBINS // n_mod
    rows = round_up(NBINS, 16)
    chunk = min(1024, pixels)
    shape = jax.ShapeDtypeStruct
    all_bins = pixel_bin.reshape(1, n_mod * pixels)
    bins = lax.dynamic_slice_in_dim(pixel_bin, module * pixels, pixels).reshape(1, pixels)
    flops = 2 * rows * pixels * 256

    partial = call(
        functools.partial(totals_kernel, chunk=chunk), shape((rows, frames), F32), bins, intensity,
        flops=flops,
    )
    others = [swap(partial, "mod", s) for s in range(1, n_mod)]
    counts, flipped = call(
        functools.partial(prepare_kernel, chunk=chunk),
        (shape((rows, 128), F32), shape((frames, pixels), BF16)),
        all_bins, intensity, flops=flops,
    )
    pooled = call(
        functools.partial(pool_kernel, chunk=chunk), shape((TBIN, pixels), BF16),
        bins, counts, flipped, partial, *others, flops=flops,
    )
    every = gather_blocks(pooled)
    stride = round_up(bins_owned, 8)
    owner = bins // bins_owned
    placed = (owner ^ module) * stride + (bins - owner * bins_owned)
    group = min(32, every.shape[0])
    grams = [
        call(
            functools.partial(gram_kernel, chunk=chunk),
            shape((n_mod * stride, TBIN * group), F32),
            placed, pooled, every[g : g + group], flops=flops,
        ).reshape(n_mod, stride, TBIN, group)
        for g in range(0, every.shape[0], group)
    ]
    gram = grams[0] if len(grams) == 1 else jnp.concatenate(grams, axis=3)
    gram = gram.reshape(n_mod, stride, TBIN * every.shape[0])
    total = gram[0]
    for s in range(1, n_mod):
        total = total + swap(gram[s], "mod", s)
    own_counts = lax.dynamic_slice_in_dim(counts, module * bins_owned, bins_owned)[:, :1]
    result = total[:bins_owned] / jnp.maximum(own_counts, 1.0)
    return result.reshape(bins_owned, TBIN, every.shape[0])


def solution(mesh):
    in_specs = (P("mod", "blk"), P())
    out_specs = P("mod", "blk", None)
    return jax.shard_map(body, mesh=mesh, in_specs=in_specs, out_specs=out_specs, check_vma=False)
```

```python
import functools

import jax
import jax.numpy as jnp
from jax import lax
from jax.experimental import pallas as pl
from jax.experimental.pallas import tpu as pltpu
from jax.sharding import PartitionSpec as P

NBINS = 200
TBIN = 4
GROUP = 8
F32 = jnp.float32
BF16 = jnp.bfloat16
NT = (((1,), (1,)), ((), ()))
TN = (((0,), (0,)), ((), ()))
VMEM = pl.BlockSpec(memory_space=pltpu.VMEM)
HBM = pl.BlockSpec(memory_space=pltpu.HBM)


def round_up(value, multiple):
    return (value + multiple - 1) // multiple * multiple


def onehot_rows(index_row, rows):
    row_ids = lax.broadcasted_iota(jnp.int32, (rows, index_row.shape[1]), 0)
    return jnp.where(row_ids == index_row, 1.0, 0.0).astype(BF16)


def split_hi_lo(value):
    hi = value.astype(BF16)
    lo = (value - hi.astype(F32)).astype(BF16)
    return hi, lo


def totals_kernel(
    bins_hbm, intensity_hbm, out_ref, onehot_ref, kept_ref, bins_ref, bins_sem, intensity_sem, *, chunk
):
    rows, pixels = onehot_ref.shape
    bins_copy = pltpu.make_async_copy(bins_hbm, bins_ref, bins_sem)
    bins_copy.start()
    intensity_copy = pltpu.make_async_copy(intensity_hbm, kept_ref, intensity_sem)
    intensity_copy.start()
    bins_copy.wait()
    module = lax.axis_index("mod")
    for start in range(0, pixels, chunk):
        part = slice(start, start + chunk)
        onehot_ref[:, part] = onehot_rows(bins_ref[module, :, part], rows)
    intensity_copy.wait()
    total = jnp.dot(onehot_ref[...], kept_ref[...], preferred_element_type=F32)
    out_ref[...] = total[: out_ref.shape[0], :]


def prepare_kernel(
    bins_ref, intensity_ref, onehot_ref, counts_ref, flipped_ref, by_pixel_ref, *, chunk
):
    rows, lanes = counts_ref.shape
    frames = intensity_ref.shape[1]
    digits = 16
    hist = jnp.zeros((digits, digits), F32)
    starts = range(0, bins_ref.shape[2], chunk)
    for module, start in [(m, start) for m in range(bins_ref.shape[0]) for start in starts]:
        piece = bins_ref[module, :, start : start + chunk]
        high = onehot_rows(piece // digits, digits)
        low = onehot_rows(piece % digits, digits)
        hist += lax.dot_general(high, low, NT, preferred_element_type=F32)
    row_ids = lax.broadcasted_iota(jnp.int32, (rows, digits), 0)
    digit_ids = lax.broadcasted_iota(jnp.int32, (rows, digits), 1)
    spread = jnp.where(row_ids // digits == digit_ids, 1.0, 0.0).astype(F32)
    by_low = jnp.dot(spread, hist, precision=lax.Precision.HIGHEST, preferred_element_type=F32)
    counts = jnp.sum(jnp.where(row_ids % digits == digit_ids, by_low, 0.0), axis=1, keepdims=True)
    counts_ref[...] = jnp.broadcast_to(counts, (rows, lanes))
    eye = (
        lax.broadcasted_iota(jnp.int32, (frames, frames), 0)
        == lax.broadcasted_iota(jnp.int32, (frames, frames), 1)
    )
    eye = jnp.where(eye, 1.0, 0.0).astype(BF16)
    for start in range(0, intensity_ref.shape[0], chunk):
        block = intensity_ref[start : start + chunk, :]
        flipped_ref[:, start : start + chunk] = lax.dot_general(
            eye, block, NT, preferred_element_type=F32
        )
        by_pixel_ref[start : start + chunk, :] = onehot_ref[:, start : start + chunk].T


def pool_kernel(counts_ref, onehot_ref, flipped_ref, own_ref, *rest, chunk):
    *other_refs, out_ref = rest
    rows = onehot_ref.shape[0]
    frames, pixels = flipped_ref.shape
    totals = own_ref[...]
    for other in other_refs:
        totals += other[...]
    totals = jnp.concatenate([totals, jnp.ones((rows - totals.shape[0], frames), F32)], axis=0)
    pool = frames // out_ref.shape[0]
    weights = counts_ref[...] / (totals * float(pool))
    hi, lo = split_hi_lo(weights)
    both = jnp.concatenate([hi, lo], axis=1)
    for start in range(0, pixels, chunk):
        part = slice(start, start + chunk)
        spread = lax.dot_general(both, onehot_ref[:, part], TN, preferred_element_type=F32)
        ratios = flipped_ref[:, part] * (spread[:frames, :] + spread[frames:, :])
        pooled = [
            jnp.sum(ratios[i * pool : (i + 1) * pool, :], axis=0, keepdims=True)
            for i in range(out_ref.shape[0])
        ]
        out_ref[:, part] = jnp.concatenate(pooled, axis=0).astype(BF16)


def gram_part(by_pixel_ref, own_ref, piece_refs, chunk):
    width = TBIN * TBIN * len(piece_refs)
    acc = jnp.zeros((2 * width, by_pixel_ref.shape[1]), F32)
    for start in range(0, by_pixel_ref.shape[0], chunk):
        part = slice(start, start + chunk)
        own = own_ref[:, part].astype(F32)
        every = jnp.concatenate([ref[:, part].astype(F32) for ref in piece_refs], axis=0)
        his, los = [], []
        for i in range(TBIN):
            hi, lo = split_hi_lo(own[i : i + 1, :] * every)
            his.append(hi)
            los.append(lo)
        products = jnp.concatenate(his + los, axis=0)
        acc += jnp.dot(products, by_pixel_ref[part, :], preferred_element_type=F32)
    return acc[:width, :] + acc[width:, :]


def gram_first_kernel(by_pixel_ref, own_ref, *rest, chunk):
    *piece_refs, out_ref = rest
    out_ref[...] = gram_part(by_pixel_ref, own_ref, piece_refs, chunk)


def gram_second_kernel(by_pixel_ref, own_ref, first_ref, *rest, n_mod, chunk):
    piece_refs, out_refs, whole_ref = rest[: -n_mod - 1], rest[-n_mod - 1 : -1], rest[-1]
    second = gram_part(by_pixel_ref, own_ref, piece_refs, chunk)
    whole_ref[...] = jnp.concatenate([first_ref[...], second], axis=0).T
    module = lax.axis_index("mod")
    owned = out_refs[0].shape[0]
    for s in range(n_mod):
        out_refs[s][...] = whole_ref[pl.ds((module ^ s) * owned, owned), :]


def final_kernel(counts_ref, *rest, distances):
    *in_refs, out_ref = rest
    owned, lanes = in_refs[0].shape
    total = in_refs[0][...]
    for ref in in_refs[1:]:
        total += ref[...]
    counts = counts_ref[pl.ds(lax.axis_index("mod") * owned, owned), :]
    total = total / jnp.maximum(counts, 1.0)
    out_row = lax.broadcasted_iota(jnp.int32, (lanes, lanes), 0)
    lane = lax.broadcasted_iota(jnp.int32, (lanes, lanes), 1)
    pieces = len(distances[0])
    per_half = TBIN * TBIN * pieces
    half, i = lane // per_half, lane % per_half // (TBIN * pieces)
    piece, row = lane % (TBIN * pieces) // TBIN, lane % TBIN
    block = jnp.zeros_like(lane)
    for h in range(2):
        for n in range(pieces):
            block = jnp.where((half == h) & (piece == n), distances[h][n], block)
    if pieces * 2 == lax.axis_size("blk"):
        block ^= lax.axis_index("blk")
    place = jnp.where(out_row == i * (TBIN * GROUP) + block * TBIN + row, 1.0, 0.0).astype(F32)
    out_ref[...] = lax.dot_general(
        place, total, NT, precision=lax.Precision.HIGHEST, preferred_element_type=F32
    )


def call(kernel, outs, *args, flops, in_specs=None, out_specs=None, scratch=()):
    moved = sum(a.size * a.dtype.itemsize for a in args)
    moved += sum(s.size * s.dtype.itemsize for s in outs)
    result = pl.pallas_call(
        kernel,
        out_shape=tuple(outs),
        in_specs=in_specs or [VMEM] * len(args),
        out_specs=out_specs or (VMEM,) * len(outs),
        scratch_shapes=list(scratch),
        compiler_params=pltpu.CompilerParams(vmem_limit_bytes=32 << 20),
        cost_estimate=pl.CostEstimate(flops=flops, bytes_accessed=moved, transcendentals=0),
    )(*args)
    return result if len(outs) > 1 else result[0]


def swap(value, axis, distance):
    size = lax.axis_size(axis)
    return lax.ppermute(value, axis, [(i, i ^ distance) for i in range(size)])


def body(intensity, pixel_bin):
    n_mod = lax.axis_size("mod")
    pixels, frames = intensity.shape
    bins_owned = NBINS // n_mod
    rows = round_up(NBINS, 16)
    chunk = min(1024, pixels)
    shape = jax.ShapeDtypeStruct
    flops = 2 * rows * pixels * 256

    mod_order = (1, 3, 2) if n_mod == 4 else tuple(range(1, n_mod))
    partial, onehot, kept, bins = call(
        functools.partial(totals_kernel, chunk=chunk),
        [
            shape((NBINS, frames), F32),
            shape((rows, pixels), BF16),
            shape((pixels, frames), BF16),
            shape((n_mod, 1, pixels), jnp.int32),
        ],
        pltpu.with_memory_space_constraint(pixel_bin.reshape(n_mod, 1, pixels), pltpu.HBM),
        pltpu.with_memory_space_constraint(intensity, pltpu.HBM),
        flops=flops, in_specs=[HBM, HBM],
        scratch=[pltpu.SemaphoreType.DMA, pltpu.SemaphoreType.DMA],
    )
    others = [swap(partial, "mod", s) for s in mod_order]
    counts, flipped, by_pixel = call(
        functools.partial(prepare_kernel, chunk=chunk),
        [shape((rows, 128), F32), shape((frames, pixels), F32), shape((pixels, rows), BF16)],
        bins, kept, onehot, flops=flops,
    )
    pooled = call(
        functools.partial(pool_kernel, chunk=chunk), [shape((TBIN, pixels), BF16)],
        counts, onehot, flipped, partial, *others, flops=flops,
    )
    width = TBIN * TBIN * GROUP
    if lax.axis_size("blk") == GROUP:
        far = [swap(pooled, "blk", s) for s in (2, 6, 4)]
        near = swap(pooled, "blk", 1)
        passed = [swap(piece, "blk", 1) for piece in far]
        groups = [([pooled, *far], [near, *passed])]
        distances = ((0, 2, 6, 4), (1, 3, 7, 5))
    else:
        every = lax.all_gather(pooled, "blk", axis=0)
        blocks = [every[b] for b in range(every.shape[0])]
        half = GROUP // 2
        groups = [
            (blocks[g : g + half], blocks[g + half : g + GROUP]) for g in range(0, len(blocks), GROUP)
        ]
        distances = (tuple(range(half)), tuple(range(half, GROUP)))
    results = []
    for first_pieces, second_pieces in groups:
        first = call(
            functools.partial(gram_first_kernel, chunk=2 * chunk), [shape((width // 2, rows), F32)],
            by_pixel, pooled, *first_pieces, flops=flops,
        )
        blocks = call(
            functools.partial(gram_second_kernel, n_mod=n_mod, chunk=2 * chunk),
            [shape((bins_owned, width), F32)] * n_mod,
            by_pixel, pooled, first, *second_pieces, flops=flops,
            scratch=[pltpu.VMEM((rows, width), F32)],
        )
        arrived = [swap(blocks[s], "mod", s) for s in mod_order]
        columns = call(
            functools.partial(final_kernel, distances=distances),
            [shape((width, bins_owned), F32)], counts, blocks[0], *arrived, flops=flops // 64,
        )
        results.append(columns.reshape(TBIN, TBIN * GROUP, bins_owned))
    result = results[0] if len(results) == 1 else jnp.concatenate(results, axis=1)
    return jnp.transpose(result, (2, 0, 1))


def solution(mesh):
    in_specs = (P("mod", "blk"), P())
    out_specs = P("mod", "blk", None)
    return jax.shard_map(body, mesh=mesh, in_specs=in_specs, out_specs=out_specs, check_vma=False)
```

```python
import functools
import math

import jax
import jax.numpy as jnp
from jax import lax
from jax.experimental import pallas as pl
from jax.experimental.pallas import tpu as pltpu
from jax.sharding import PartitionSpec as P

NBINS = 200
TBIN = 4
GROUP = 8
MAX_INTENSITY = 820.0
MAX_HALF = 65504.0
F32 = jnp.float32
BF16 = jnp.bfloat16
NT = (((1,), (1,)), ((), ()))
TN = (((0,), (0,)), ((), ()))
VMEM = pl.BlockSpec(memory_space=pltpu.VMEM)
HBM = pl.BlockSpec(memory_space=pltpu.HBM)


def round_up(value, multiple):
    return (value + multiple - 1) // multiple * multiple


def onehot_rows(index_row, rows):
    row_ids = lax.broadcasted_iota(jnp.int32, (rows, index_row.shape[1]), 0)
    return jnp.where(row_ids == index_row, 1.0, 0.0).astype(BF16)


def split_hi_lo(value):
    hi = value.astype(BF16)
    lo = (value - hi.astype(F32)).astype(BF16)
    return hi, lo


def totals_kernel(
    bins_hbm, intensity_hbm, out_ref, onehot_ref, kept_ref, bins_ref, bins_sem, intensity_sem, *, chunk
):
    rows, pixels = onehot_ref.shape
    bins_copy = pltpu.make_async_copy(bins_hbm, bins_ref, bins_sem)
    bins_copy.start()
    intensity_copy = pltpu.make_async_copy(intensity_hbm, kept_ref, intensity_sem)
    intensity_copy.start()
    bins_copy.wait()
    module = lax.axis_index("mod")
    for start in range(0, pixels, chunk):
        part = slice(start, start + chunk)
        onehot_ref[:, part] = onehot_rows(bins_ref[module, :, part], rows)
    intensity_copy.wait()
    total = jnp.dot(onehot_ref[...], kept_ref[...], preferred_element_type=F32)
    out_ref[...] = total[: out_ref.shape[0], :]


def prepare_kernel(
    bins_ref, intensity_ref, onehot_ref, counts_ref, flipped_ref, by_pixel_ref, *, chunk
):
    rows, lanes = counts_ref.shape
    frames = intensity_ref.shape[1]
    digits = 16
    hist = jnp.zeros((digits, digits), F32)
    starts = range(0, bins_ref.shape[2], chunk)
    for module, start in [(m, start) for m in range(bins_ref.shape[0]) for start in starts]:
        piece = bins_ref[module, :, start : start + chunk]
        high = onehot_rows(piece // digits, digits)
        low = onehot_rows(piece % digits, digits)
        hist += lax.dot_general(high, low, NT, preferred_element_type=F32)
    row_ids = lax.broadcasted_iota(jnp.int32, (rows, digits), 0)
    digit_ids = lax.broadcasted_iota(jnp.int32, (rows, digits), 1)
    spread = jnp.where(row_ids // digits == digit_ids, 1.0, 0.0).astype(F32)
    by_low = jnp.dot(spread, hist, precision=lax.Precision.HIGHEST, preferred_element_type=F32)
    counts = jnp.sum(jnp.where(row_ids % digits == digit_ids, by_low, 0.0), axis=1, keepdims=True)
    counts_ref[...] = jnp.broadcast_to(counts, (rows, lanes))
    eye = (
        lax.broadcasted_iota(jnp.int32, (frames, frames), 0)
        == lax.broadcasted_iota(jnp.int32, (frames, frames), 1)
    )
    eye = jnp.where(eye, 1.0, 0.0).astype(BF16)
    for start in range(0, intensity_ref.shape[0], chunk):
        block = intensity_ref[start : start + chunk, :]
        flipped_ref[:, start : start + chunk] = lax.dot_general(
            eye, block, NT, preferred_element_type=F32
        )
        by_pixel_ref[start : start + chunk, :] = onehot_ref[:, start : start + chunk].T


def pool_kernel(counts_ref, onehot_ref, flipped_ref, own_ref, *rest, chunk):
    *other_refs, out_ref = rest
    rows = onehot_ref.shape[0]
    frames, pixels = flipped_ref.shape
    totals = own_ref[...]
    for other in other_refs:
        totals += other[...]
    totals = jnp.concatenate([totals, jnp.ones((rows - totals.shape[0], frames), F32)], axis=0)
    pool = frames // out_ref.shape[0]
    weights = counts_ref[...] / (totals * float(pool))
    hi, lo = split_hi_lo(weights)
    both = jnp.concatenate([hi, lo], axis=1)
    for start in range(0, pixels, chunk):
        part = slice(start, start + chunk)
        spread = lax.dot_general(both, onehot_ref[:, part], TN, preferred_element_type=F32)
        ratios = flipped_ref[:, part] * (spread[:frames, :] + spread[frames:, :])
        pooled = [
            jnp.sum(ratios[i * pool : (i + 1) * pool, :], axis=0, keepdims=True)
            for i in range(out_ref.shape[0])
        ]
        out_ref[:, part] = jnp.concatenate(pooled, axis=0).astype(BF16)


def gram_part(by_pixel_ref, own_ref, piece_refs, chunk):
    width = TBIN * TBIN * len(piece_refs)
    acc = jnp.zeros((2 * width, by_pixel_ref.shape[1]), F32)
    for start in range(0, by_pixel_ref.shape[0], chunk):
        part = slice(start, start + chunk)
        own = own_ref[:, part].astype(F32)
        every = jnp.concatenate([ref[:, part].astype(F32) for ref in piece_refs], axis=0)
        his, los = [], []
        for i in range(TBIN):
            hi, lo = split_hi_lo(own[i : i + 1, :] * every)
            his.append(hi)
            los.append(lo)
        products = jnp.concatenate(his + los, axis=0)
        acc += jnp.dot(products, by_pixel_ref[part, :], preferred_element_type=F32)
    return acc[:width, :] + acc[width:, :]


def gram_first_kernel(by_pixel_ref, own_ref, *rest, chunk):
    *piece_refs, out_ref = rest
    out_ref[...] = gram_part(by_pixel_ref, own_ref, piece_refs, chunk)


def gram_second_kernel(by_pixel_ref, own_ref, first_ref, *rest, n_mod, chunk):
    piece_refs, out_refs, whole_ref = rest[: -n_mod - 1], rest[-n_mod - 1 : -1], rest[-1]
    second = gram_part(by_pixel_ref, own_ref, piece_refs, chunk)
    whole_ref[...] = jnp.concatenate([first_ref[...], second], axis=0).T
    module = lax.axis_index("mod")
    owned = out_refs[0].shape[0]
    for s in range(n_mod):
        out_refs[s][...] = whole_ref[pl.ds((module ^ s) * owned, owned), :]


def final_kernel(counts_ref, *rest, distances):
    *in_refs, out_ref = rest
    owned, lanes = in_refs[0].shape
    total = in_refs[0][...]
    for ref in in_refs[1:]:
        total += ref[...]
    counts = counts_ref[pl.ds(lax.axis_index("mod") * owned, owned), :]
    total = total / jnp.maximum(counts, 1.0)
    out_row = lax.broadcasted_iota(jnp.int32, (lanes, lanes), 0)
    lane = lax.broadcasted_iota(jnp.int32, (lanes, lanes), 1)
    pieces = len(distances[0])
    per_half = TBIN * TBIN * pieces
    half, i = lane // per_half, lane % per_half // (TBIN * pieces)
    piece, row = lane % (TBIN * pieces) // TBIN, lane % TBIN
    block = jnp.zeros_like(lane)
    for h in range(2):
        for n in range(pieces):
            block = jnp.where((half == h) & (piece == n), distances[h][n], block)
    if pieces * 2 == lax.axis_size("blk"):
        block ^= lax.axis_index("blk")
    place = jnp.where(out_row == i * (TBIN * GROUP) + block * TBIN + row, 1.0, 0.0).astype(F32)
    out_ref[...] = lax.dot_general(
        place, total, NT, precision=lax.Precision.HIGHEST, preferred_element_type=F32
    )


def call(kernel, outs, *args, flops, in_specs=None, out_specs=None, scratch=()):
    moved = sum(a.size * a.dtype.itemsize for a in args)
    moved += sum(s.size * s.dtype.itemsize for s in outs)
    result = pl.pallas_call(
        kernel,
        out_shape=tuple(outs),
        in_specs=in_specs or [VMEM] * len(args),
        out_specs=out_specs or (VMEM,) * len(outs),
        scratch_shapes=list(scratch),
        compiler_params=pltpu.CompilerParams(vmem_limit_bytes=32 << 20),
        cost_estimate=pl.CostEstimate(flops=flops, bytes_accessed=moved, transcendentals=0),
    )(*args)
    return result if len(outs) > 1 else result[0]


def swap(value, axis, distance):
    size = lax.axis_size(axis)
    return lax.ppermute(value, axis, [(i, i ^ distance) for i in range(size)])


def body(intensity, pixel_bin):
    n_mod = lax.axis_size("mod")
    pixels, frames = intensity.shape
    bins_owned = NBINS // n_mod
    rows = round_up(NBINS, 16)
    chunk = min(1024, pixels)
    shape = jax.ShapeDtypeStruct
    flops = 2 * rows * pixels * 256

    mod_order = tuple(range(1, n_mod))
    partial, onehot, kept, bins = call(
        functools.partial(totals_kernel, chunk=chunk),
        [
            shape((NBINS, frames), F32),
            shape((rows, pixels), BF16),
            shape((pixels, frames), BF16),
            shape((n_mod, 1, pixels), jnp.int32),
        ],
        pltpu.with_memory_space_constraint(pixel_bin.reshape(n_mod, 1, pixels), pltpu.HBM),
        pltpu.with_memory_space_constraint(intensity, pltpu.HBM),
        flops=flops, in_specs=[HBM, HBM],
        scratch=[pltpu.SemaphoreType.DMA, pltpu.SemaphoreType.DMA],
    )
    scale = 2.0 ** math.ceil(math.log2(MAX_INTENSITY * pixels / MAX_HALF))
    sent = (partial * (1.0 / scale)).astype(jnp.float16)
    others = [swap(sent, "mod", s).astype(F32) * scale for s in mod_order]
    counts, flipped, by_pixel = call(
        functools.partial(prepare_kernel, chunk=chunk),
        [shape((rows, 128), F32), shape((frames, pixels), F32), shape((pixels, rows), BF16)],
        bins, kept, onehot, flops=flops,
    )
    pooled = call(
        functools.partial(pool_kernel, chunk=chunk), [shape((TBIN, pixels), BF16)],
        counts, onehot, flipped, partial, *others, flops=flops,
    )
    width = TBIN * TBIN * GROUP
    if lax.axis_size("blk") == GROUP:
        far = [swap(pooled, "blk", s) for s in (2, 6, 4)]
        near = swap(pooled, "blk", 1)
        passed = [swap(piece, "blk", 1) for piece in far]
        groups = [([pooled, *far], [near, *passed])]
        distances = ((0, 2, 6, 4), (1, 3, 7, 5))
    else:
        every = lax.all_gather(pooled, "blk", axis=0)
        blocks = [every[b] for b in range(every.shape[0])]
        half = GROUP // 2
        groups = [
            (blocks[g : g + half], blocks[g + half : g + GROUP]) for g in range(0, len(blocks), GROUP)
        ]
        distances = (tuple(range(half)), tuple(range(half, GROUP)))
    results = []
    for first_pieces, second_pieces in groups:
        first = call(
            functools.partial(gram_first_kernel, chunk=2 * chunk), [shape((width // 2, rows), F32)],
            by_pixel, pooled, *first_pieces, flops=flops,
        )
        blocks = call(
            functools.partial(gram_second_kernel, n_mod=n_mod, chunk=2 * chunk),
            [shape((bins_owned, width), F32)] * n_mod,
            by_pixel, pooled, first, *second_pieces, flops=flops,
            scratch=[pltpu.VMEM((rows, width), F32)],
        )
        arrived = [swap(blocks[s], "mod", s) for s in mod_order]
        columns = call(
            functools.partial(final_kernel, distances=distances),
            [shape((width, bins_owned), F32)], counts, blocks[0], *arrived, flops=flops // 64,
        )
        results.append(columns.reshape(TBIN, TBIN * GROUP, bins_owned))
    result = results[0] if len(results) == 1 else jnp.concatenate(results, axis=1)
    return jnp.transpose(result, (2, 0, 1))


def solution(mesh):
    in_specs = (P("mod", "blk"), P())
    out_specs = P("mod", "blk", None)
    return jax.shard_map(body, mesh=mesh, in_specs=in_specs, out_specs=out_specs, check_vma=False)
```

```python
import functools
import math

import jax
import jax.numpy as jnp
from jax import lax
from jax.experimental import pallas as pl
from jax.experimental.pallas import tpu as pltpu
from jax.sharding import PartitionSpec as P

NBINS = 200
TBIN = 4
GROUP = 8
MAX_INTENSITY = 820.0
MAX_HALF = 65504.0
F32 = jnp.float32
BF16 = jnp.bfloat16
NT = (((1,), (1,)), ((), ()))
TN = (((0,), (0,)), ((), ()))
VMEM = pl.BlockSpec(memory_space=pltpu.VMEM)
HBM = pl.BlockSpec(memory_space=pltpu.HBM)


def round_up(value, multiple):
    return (value + multiple - 1) // multiple * multiple


def onehot_rows(index_row, rows):
    row_ids = lax.broadcasted_iota(jnp.int32, (rows, index_row.shape[1]), 0)
    return jnp.where(row_ids == index_row, 1.0, 0.0).astype(BF16)


def split_hi_lo(value):
    hi = value.astype(BF16)
    lo = (value - hi.astype(F32)).astype(BF16)
    return hi, lo


def totals_kernel(
    bins_hbm, intensity_hbm, out_ref, onehot_ref, kept_ref, bins_ref, bins_sem, intensity_sem, *, chunk
):
    rows, pixels = onehot_ref.shape
    bins_copy = pltpu.make_async_copy(bins_hbm, bins_ref, bins_sem)
    bins_copy.start()
    intensity_copy = pltpu.make_async_copy(intensity_hbm, kept_ref, intensity_sem)
    intensity_copy.start()
    bins_copy.wait()
    module = lax.axis_index("mod")
    for start in range(0, pixels, chunk):
        part = slice(start, start + chunk)
        onehot_ref[:, part] = onehot_rows(bins_ref[module, :, part], rows)
    intensity_copy.wait()
    total = jnp.dot(onehot_ref[...], kept_ref[...], preferred_element_type=F32)
    out_ref[...] = total[: out_ref.shape[0], :]


def prepare_kernel(
    bins_ref, intensity_ref, counts_ref, flipped_ref, *, chunk
):
    rows, lanes = counts_ref.shape
    frames = intensity_ref.shape[1]
    digits = 16
    hist = jnp.zeros((digits, digits), F32)
    starts = range(0, bins_ref.shape[2], chunk)
    for module, start in [(m, start) for m in range(bins_ref.shape[0]) for start in starts]:
        piece = bins_ref[module, :, start : start + chunk]
        high = onehot_rows(piece // digits, digits)
        low = onehot_rows(piece % digits, digits)
        hist += lax.dot_general(high, low, NT, preferred_element_type=F32)
    row_ids = lax.broadcasted_iota(jnp.int32, (rows, digits), 0)
    digit_ids = lax.broadcasted_iota(jnp.int32, (rows, digits), 1)
    spread = jnp.where(row_ids // digits == digit_ids, 1.0, 0.0).astype(F32)
    by_low = jnp.dot(spread, hist, precision=lax.Precision.HIGHEST, preferred_element_type=F32)
    counts = jnp.sum(jnp.where(row_ids % digits == digit_ids, by_low, 0.0), axis=1, keepdims=True)
    counts_ref[...] = jnp.broadcast_to(counts, (rows, lanes))
    eye = (
        lax.broadcasted_iota(jnp.int32, (frames, frames), 0)
        == lax.broadcasted_iota(jnp.int32, (frames, frames), 1)
    )
    eye = jnp.where(eye, 1.0, 0.0).astype(BF16)
    for start in range(0, intensity_ref.shape[0], chunk):
        block = intensity_ref[start : start + chunk, :]
        flipped_ref[:, start : start + chunk] = lax.dot_general(
            eye, block, NT, preferred_element_type=F32
        )


def by_pixel_kernel(onehot_ref, after_ref, out_ref, *, chunk):
    del after_ref
    for start in range(0, out_ref.shape[0], chunk):
        part = slice(start, start + chunk)
        out_ref[part, :] = onehot_ref[:, part].T


def pool_kernel(counts_ref, onehot_ref, flipped_ref, own_ref, *rest, chunk):
    *other_refs, out_ref = rest
    rows = onehot_ref.shape[0]
    frames, pixels = flipped_ref.shape
    totals = own_ref[...]
    for other in other_refs:
        totals += other[...]
    totals = jnp.concatenate([totals, jnp.ones((rows - totals.shape[0], frames), F32)], axis=0)
    pool = frames // out_ref.shape[0]
    weights = counts_ref[...] / (totals * float(pool))
    hi, lo = split_hi_lo(weights)
    both = jnp.concatenate([hi, lo], axis=1)
    for start in range(0, pixels, chunk):
        part = slice(start, start + chunk)
        spread = lax.dot_general(both, onehot_ref[:, part], TN, preferred_element_type=F32)
        ratios = flipped_ref[:, part] * (spread[:frames, :] + spread[frames:, :])
        pooled = [
            jnp.sum(ratios[i * pool : (i + 1) * pool, :], axis=0, keepdims=True)
            for i in range(out_ref.shape[0])
        ]
        out_ref[:, part] = jnp.concatenate(pooled, axis=0).astype(BF16)


def gram_part(by_pixel_ref, own_ref, piece_refs, chunk):
    width = TBIN * TBIN * len(piece_refs)
    acc = jnp.zeros((2 * width, by_pixel_ref.shape[1]), F32)
    for start in range(0, by_pixel_ref.shape[0], chunk):
        part = slice(start, start + chunk)
        own = own_ref[:, part].astype(F32)
        every = jnp.concatenate([ref[:, part].astype(F32) for ref in piece_refs], axis=0)
        his, los = [], []
        for i in range(TBIN):
            hi, lo = split_hi_lo(own[i : i + 1, :] * every)
            his.append(hi)
            los.append(lo)
        products = jnp.concatenate(his + los, axis=0)
        acc += jnp.dot(products, by_pixel_ref[part, :], preferred_element_type=F32)
    return acc[:width, :] + acc[width:, :]


def gram_first_kernel(by_pixel_ref, own_ref, *rest, chunk):
    *piece_refs, out_ref = rest
    out_ref[...] = gram_part(by_pixel_ref, own_ref, piece_refs, chunk)


def gram_second_kernel(by_pixel_ref, own_ref, first_ref, *rest, n_mod, chunk):
    piece_refs, out_refs, whole_ref = rest[: -n_mod - 1], rest[-n_mod - 1 : -1], rest[-1]
    second = gram_part(by_pixel_ref, own_ref, piece_refs, chunk)
    whole_ref[...] = jnp.concatenate([first_ref[...], second], axis=0).T
    module = lax.axis_index("mod")
    owned = out_refs[0].shape[0]
    for s in range(n_mod):
        out_refs[s][...] = whole_ref[pl.ds((module ^ s) * owned, owned), :]


def final_kernel(counts_ref, *rest, distances):
    *in_refs, out_ref = rest
    owned, lanes = in_refs[0].shape
    total = in_refs[0][...]
    for ref in in_refs[1:]:
        total += ref[...]
    counts = counts_ref[pl.ds(lax.axis_index("mod") * owned, owned), :]
    total = total / jnp.maximum(counts, 1.0)
    out_row = lax.broadcasted_iota(jnp.int32, (lanes, lanes), 0)
    lane = lax.broadcasted_iota(jnp.int32, (lanes, lanes), 1)
    pieces = len(distances[0])
    per_half = TBIN * TBIN * pieces
    half, i = lane // per_half, lane % per_half // (TBIN * pieces)
    piece, row = lane % (TBIN * pieces) // TBIN, lane % TBIN
    block = jnp.zeros_like(lane)
    for h in range(2):
        for n in range(pieces):
            block = jnp.where((half == h) & (piece == n), distances[h][n], block)
    if pieces * 2 == lax.axis_size("blk"):
        block ^= lax.axis_index("blk")
    place = jnp.where(out_row == i * (TBIN * GROUP) + block * TBIN + row, 1.0, 0.0).astype(F32)
    out_ref[...] = lax.dot_general(
        place, total, NT, precision=lax.Precision.HIGHEST, preferred_element_type=F32
    )


def call(kernel, outs, *args, flops, in_specs=None, out_specs=None, scratch=()):
    moved = sum(a.size * a.dtype.itemsize for a in args)
    moved += sum(s.size * s.dtype.itemsize for s in outs)
    result = pl.pallas_call(
        kernel,
        out_shape=tuple(outs),
        in_specs=in_specs or [VMEM] * len(args),
        out_specs=out_specs or (VMEM,) * len(outs),
        scratch_shapes=list(scratch),
        compiler_params=pltpu.CompilerParams(vmem_limit_bytes=32 << 20),
        cost_estimate=pl.CostEstimate(flops=flops, bytes_accessed=moved, transcendentals=0),
    )(*args)
    return result if len(outs) > 1 else result[0]


def swap(value, axis, distance):
    size = lax.axis_size(axis)
    return lax.ppermute(value, axis, [(i, i ^ distance) for i in range(size)])


def body(intensity, pixel_bin):
    n_mod = lax.axis_size("mod")
    pixels, frames = intensity.shape
    bins_owned = NBINS // n_mod
    rows = round_up(NBINS, 16)
    chunk = min(1024, pixels)
    shape = jax.ShapeDtypeStruct
    flops = 2 * rows * pixels * 256

    mod_order = tuple(range(1, n_mod))
    last_order = mod_order[::-1]
    partial, onehot, kept, bins = call(
        functools.partial(totals_kernel, chunk=chunk),
        [
            shape((NBINS, frames), F32),
            shape((rows, pixels), BF16),
            shape((pixels, frames), BF16),
            shape((n_mod, 1, pixels), jnp.int32),
        ],
        pltpu.with_memory_space_constraint(pixel_bin.reshape(n_mod, 1, pixels), pltpu.HBM),
        pltpu.with_memory_space_constraint(intensity, pltpu.HBM),
        flops=flops, in_specs=[HBM, HBM],
        scratch=[pltpu.SemaphoreType.DMA, pltpu.SemaphoreType.DMA],
    )
    scale = 2.0 ** math.ceil(math.log2(MAX_INTENSITY * pixels / MAX_HALF))
    sent = (partial * (1.0 / scale)).astype(jnp.float16)
    others = [swap(sent, "mod", s).astype(F32) * scale for s in mod_order]
    counts, flipped = call(
        functools.partial(prepare_kernel, chunk=chunk),
        [shape((rows, 128), F32), shape((frames, pixels), F32)],
        bins, kept, flops=flops,
    )
    pooled = call(
        functools.partial(pool_kernel, chunk=chunk), [shape((TBIN, pixels), BF16)],
        counts, onehot, flipped, partial, *others, flops=flops,
    )
    by_pixel = call(
        functools.partial(by_pixel_kernel, chunk=chunk), [shape((pixels, rows), BF16)],
        onehot, pooled, flops=flops,
    )
    width = TBIN * TBIN * GROUP
    if lax.axis_size("blk") == GROUP:
        far = [swap(pooled, "blk", s) for s in (6,2,4)]
        near = swap(pooled, "blk", 1)
        passed = [swap(piece, "blk", 1) for piece in far]
        groups = [([pooled, *far], [near, *passed])]
        distances = ((0, 6, 2, 4), (1, 7, 3, 5))
    else:
        every = lax.all_gather(pooled, "blk", axis=0)
        blocks = [every[b] for b in range(every.shape[0])]
        half = GROUP // 2
        groups = [
            (blocks[g : g + half], blocks[g + half : g + GROUP]) for g in range(0, len(blocks), GROUP)
        ]
        distances = (tuple(range(half)), tuple(range(half, GROUP)))
    results = []
    for first_pieces, second_pieces in groups:
        first = call(
            functools.partial(gram_first_kernel, chunk=2 * chunk), [shape((width // 2, rows), F32)],
            by_pixel, pooled, *first_pieces, flops=flops,
        )
        blocks = call(
            functools.partial(gram_second_kernel, n_mod=n_mod, chunk=2 * chunk),
            [shape((bins_owned, width), F32)] * n_mod,
            by_pixel, pooled, first, *second_pieces, flops=flops,
            scratch=[pltpu.VMEM((rows, width), F32)],
        )
        arrived = [swap(blocks[s], "mod", s) for s in last_order]
        columns = call(
            functools.partial(final_kernel, distances=distances),
            [shape((width, bins_owned), F32)], counts, blocks[0], *arrived, flops=flops // 64,
        )
        results.append(columns.reshape(TBIN, TBIN * GROUP, bins_owned))
    result = results[0] if len(results) == 1 else jnp.concatenate(results, axis=1)
    return jnp.transpose(result, (2, 0, 1))


def solution(mesh):
    in_specs = (P("mod", "blk"), P())
    out_specs = P("mod", "blk", None)
    return jax.shard_map(body, mesh=mesh, in_specs=in_specs, out_specs=out_specs, check_vma=False)
```

```python
import functools
import math

import jax
import jax.numpy as jnp
from jax import lax
from jax.experimental import pallas as pl
from jax.experimental.pallas import tpu as pltpu
from jax.sharding import PartitionSpec as P

NBINS = 200
TBIN = 4
GROUP = 8
MAX_INTENSITY = 820.0
MAX_HALF = 65504.0
F32 = jnp.float32
BF16 = jnp.bfloat16
NT = (((1,), (1,)), ((), ()))
TN = (((0,), (0,)), ((), ()))
VMEM = pl.BlockSpec(memory_space=pltpu.VMEM)
HBM = pl.BlockSpec(memory_space=pltpu.HBM)


def round_up(value, multiple):
    return (value + multiple - 1) // multiple * multiple


def onehot_rows(index_row, rows):
    row_ids = lax.broadcasted_iota(jnp.int32, (rows, index_row.shape[1]), 0)
    return jnp.where(row_ids == index_row, 1.0, 0.0).astype(BF16)


def split_hi_lo(value):
    hi = value.astype(BF16)
    lo = (value - hi.astype(F32)).astype(BF16)
    return hi, lo


def totals_kernel(
    bins_hbm, intensity_hbm, out_ref, onehot_ref, kept_ref, bins_ref, bins_sem, intensity_sem, *, chunk
):
    rows, pixels = onehot_ref.shape
    bins_copy = pltpu.make_async_copy(bins_hbm, bins_ref, bins_sem)
    bins_copy.start()
    intensity_copy = pltpu.make_async_copy(intensity_hbm, kept_ref, intensity_sem)
    intensity_copy.start()
    bins_copy.wait()
    module = lax.axis_index("mod")
    for start in range(0, pixels, chunk):
        part = slice(start, start + chunk)
        onehot_ref[:, part] = onehot_rows(bins_ref[module, :, part], rows)
    intensity_copy.wait()
    total = jnp.dot(onehot_ref[...], kept_ref[...], preferred_element_type=F32)
    out_ref[...] = total[: out_ref.shape[0], :]


def prepare_kernel(
    bins_ref, intensity_ref, counts_ref, flipped_ref, *, chunk
):
    rows, lanes = counts_ref.shape
    frames = intensity_ref.shape[1]
    digits = 16
    hist = jnp.zeros((digits, digits), F32)
    starts = range(0, bins_ref.shape[2], chunk)
    for module, start in [(m, start) for m in range(bins_ref.shape[0]) for start in starts]:
        piece = bins_ref[module, :, start : start + chunk]
        high = onehot_rows(piece // digits, digits)
        low = onehot_rows(piece % digits, digits)
        hist += lax.dot_general(high, low, NT, preferred_element_type=F32)
    row_ids = lax.broadcasted_iota(jnp.int32, (rows, digits), 0)
    digit_ids = lax.broadcasted_iota(jnp.int32, (rows, digits), 1)
    spread = jnp.where(row_ids // digits == digit_ids, 1.0, 0.0).astype(F32)
    by_low = jnp.dot(spread, hist, precision=lax.Precision.HIGHEST, preferred_element_type=F32)
    counts = jnp.sum(jnp.where(row_ids % digits == digit_ids, by_low, 0.0), axis=1, keepdims=True)
    counts_ref[...] = jnp.broadcast_to(counts, (rows, lanes))
    eye = (
        lax.broadcasted_iota(jnp.int32, (frames, frames), 0)
        == lax.broadcasted_iota(jnp.int32, (frames, frames), 1)
    )
    eye = jnp.where(eye, 1.0, 0.0).astype(BF16)
    for start in range(0, intensity_ref.shape[0], chunk):
        block = intensity_ref[start : start + chunk, :]
        flipped_ref[:, start : start + chunk] = lax.dot_general(
            eye, block, NT, preferred_element_type=F32
        )


def by_pixel_kernel(onehot_ref, after_ref, out_ref, *, chunk):
    del after_ref
    for start in range(0, out_ref.shape[0], chunk):
        part = slice(start, start + chunk)
        out_ref[part, :] = onehot_ref[:, part].T


def pool_kernel(counts_ref, onehot_ref, flipped_ref, own_ref, *rest, chunk):
    *other_refs, out_ref = rest
    rows = onehot_ref.shape[0]
    frames, pixels = flipped_ref.shape
    totals = own_ref[...]
    for other in other_refs:
        totals += other[...]
    totals = jnp.concatenate([totals, jnp.ones((rows - totals.shape[0], frames), F32)], axis=0)
    pool = frames // out_ref.shape[0]
    weights = counts_ref[...] / (totals * float(pool))
    hi, lo = split_hi_lo(weights)
    both = jnp.concatenate([hi, lo], axis=1)
    for start in range(0, pixels, chunk):
        part = slice(start, start + chunk)
        spread = lax.dot_general(both, onehot_ref[:, part], TN, preferred_element_type=F32)
        ratios = flipped_ref[:, part] * (spread[:frames, :] + spread[frames:, :])
        pooled = [
            jnp.sum(ratios[i * pool : (i + 1) * pool, :], axis=0, keepdims=True)
            for i in range(out_ref.shape[0])
        ]
        out_ref[:, part] = jnp.concatenate(pooled, axis=0).astype(BF16)


def gram_part(by_pixel_ref, own_ref, piece_refs, chunk):
    width = TBIN * TBIN * len(piece_refs)
    acc = jnp.zeros((2 * width, by_pixel_ref.shape[1]), F32)
    for start in range(0, by_pixel_ref.shape[0], chunk):
        part = slice(start, start + chunk)
        own = own_ref[:, part].astype(F32)
        every = jnp.concatenate([ref[:, part].astype(F32) for ref in piece_refs], axis=0)
        his, los = [], []
        for i in range(TBIN):
            hi, lo = split_hi_lo(own[i : i + 1, :] * every)
            his.append(hi)
            los.append(lo)
        products = jnp.concatenate(his + los, axis=0)
        acc += jnp.dot(products, by_pixel_ref[part, :], preferred_element_type=F32)
    return acc[:width, :] + acc[width:, :]


def gram_first_kernel(by_pixel_ref, own_ref, *rest, chunk):
    *piece_refs, out_ref = rest
    out_ref[...] = gram_part(by_pixel_ref, own_ref, piece_refs, chunk)


def gram_second_kernel(by_pixel_ref, own_ref, first_ref, *rest, n_mod, chunk):
    piece_refs, out_refs, whole_ref = rest[: -n_mod - 1], rest[-n_mod - 1 : -1], rest[-1]
    second = gram_part(by_pixel_ref, own_ref, piece_refs, chunk)
    whole_ref[...] = jnp.concatenate([first_ref[...], second], axis=0).T
    module = lax.axis_index("mod")
    owned = out_refs[0].shape[0]
    for s in range(n_mod):
        out_refs[s][...] = whole_ref[pl.ds((module ^ s) * owned, owned), :]


def final_kernel(counts_ref, *rest, distances):
    *in_refs, out_ref = rest
    owned, lanes = in_refs[0].shape
    total = in_refs[0][...]
    for ref in in_refs[1:]:
        total += ref[...]
    counts = counts_ref[pl.ds(lax.axis_index("mod") * owned, owned), :]
    total = total / jnp.maximum(counts, 1.0)
    out_row = lax.broadcasted_iota(jnp.int32, (lanes, lanes), 0)
    lane = lax.broadcasted_iota(jnp.int32, (lanes, lanes), 1)
    pieces = len(distances[0])
    per_half = TBIN * TBIN * pieces
    half, i = lane // per_half, lane % per_half // (TBIN * pieces)
    piece, row = lane % (TBIN * pieces) // TBIN, lane % TBIN
    block = jnp.zeros_like(lane)
    for h in range(2):
        for n in range(pieces):
            block = jnp.where((half == h) & (piece == n), distances[h][n], block)
    if pieces * 2 == lax.axis_size("blk"):
        block ^= lax.axis_index("blk")
    place = jnp.where(out_row == i * (TBIN * GROUP) + block * TBIN + row, 1.0, 0.0).astype(F32)
    place = place.astype(BF16)
    high = total.astype(BF16)
    rest = total - high.astype(F32)
    middle = rest.astype(BF16)
    low = (rest - middle.astype(F32)).astype(BF16)
    moved = [lax.dot_general(place, p, NT, preferred_element_type=F32) for p in (high, middle, low)]
    out_ref[...] = moved[0] + (moved[1] + moved[2])


def call(kernel, outs, *args, flops, in_specs=None, out_specs=None, scratch=()):
    moved = sum(a.size * a.dtype.itemsize for a in args)
    moved += sum(s.size * s.dtype.itemsize for s in outs)
    result = pl.pallas_call(
        kernel,
        out_shape=tuple(outs),
        in_specs=in_specs or [VMEM] * len(args),
        out_specs=out_specs or (VMEM,) * len(outs),
        scratch_shapes=list(scratch),
        compiler_params=pltpu.CompilerParams(vmem_limit_bytes=32 << 20),
        cost_estimate=pl.CostEstimate(flops=flops, bytes_accessed=moved, transcendentals=0),
    )(*args)
    return result if len(outs) > 1 else result[0]


def swap(value, axis, distance):
    size = lax.axis_size(axis)
    return lax.ppermute(value, axis, [(i, i ^ distance) for i in range(size)])


def body(intensity, pixel_bin):
    n_mod = lax.axis_size("mod")
    pixels, frames = intensity.shape
    bins_owned = NBINS // n_mod
    rows = round_up(NBINS, 16)
    chunk = min(1024, pixels)
    shape = jax.ShapeDtypeStruct
    flops = 2 * rows * pixels * 256

    mod_order = tuple(range(1, n_mod))
    last_order = mod_order[::-1]
    partial, onehot, kept, bins = call(
        functools.partial(totals_kernel, chunk=chunk),
        [
            shape((NBINS, frames), F32),
            shape((rows, pixels), BF16),
            shape((pixels, frames), BF16),
            shape((n_mod, 1, pixels), jnp.int32),
        ],
        pltpu.with_memory_space_constraint(pixel_bin.reshape(n_mod, 1, pixels), pltpu.HBM),
        pltpu.with_memory_space_constraint(intensity, pltpu.HBM),
        flops=flops, in_specs=[HBM, HBM],
        scratch=[pltpu.SemaphoreType.DMA, pltpu.SemaphoreType.DMA],
    )
    scale = 2.0 ** math.ceil(math.log2(MAX_INTENSITY * pixels / MAX_HALF))
    sent = (partial * (1.0 / scale)).astype(jnp.float16)
    others = [swap(sent, "mod", s).astype(F32) * scale for s in mod_order]
    counts, flipped = call(
        functools.partial(prepare_kernel, chunk=chunk),
        [shape((rows, 128), F32), shape((frames, pixels), F32)],
        bins, kept, flops=flops,
    )
    pooled = call(
        functools.partial(pool_kernel, chunk=4 * chunk), [shape((TBIN, pixels), BF16)],
        counts, onehot, flipped, partial, *others, flops=flops,
    )
    by_pixel = call(
        functools.partial(by_pixel_kernel, chunk=chunk), [shape((pixels, rows), BF16)],
        onehot, pooled, flops=flops,
    )
    width = TBIN * TBIN * GROUP
    if lax.axis_size("blk") == GROUP:
        far = [swap(pooled, "blk", s) for s in (6,2,4)]
        far[:2] = lax.optimization_barrier((far[0], far[1]))
        near = swap(lax.optimization_barrier((pooled, far[0]))[0], "blk", 1)
        passed = [swap(piece, "blk", 1) for piece in far]
        groups = [([pooled, *far], [near, *passed])]
        distances = ((0, 6, 2, 4), (1, 7, 3, 5))
    else:
        every = lax.all_gather(pooled, "blk", axis=0)
        blocks = [every[b] for b in range(every.shape[0])]
        half = GROUP // 2
        groups = [
            (blocks[g : g + half], blocks[g + half : g + GROUP]) for g in range(0, len(blocks), GROUP)
        ]
        distances = (tuple(range(half)), tuple(range(half, GROUP)))
    results = []
    for first_pieces, second_pieces in groups:
        first = call(
            functools.partial(gram_first_kernel, chunk=2 * chunk), [shape((width // 2, rows), F32)],
            by_pixel, pooled, *first_pieces, flops=flops,
        )
        blocks = call(
            functools.partial(gram_second_kernel, n_mod=n_mod, chunk=2 * chunk),
            [shape((bins_owned, width), F32)] * n_mod,
            by_pixel, pooled, first, *second_pieces, flops=flops,
            scratch=[pltpu.VMEM((rows, width), F32)],
        )
        arrived = [swap(blocks[s], "mod", s) for s in last_order]
        columns = call(
            functools.partial(final_kernel, distances=distances),
            [shape((width, bins_owned), F32)], counts, blocks[0], *arrived, flops=flops // 64,
        )
        results.append(columns.reshape(TBIN, TBIN * GROUP, bins_owned))
    result = results[0] if len(results) == 1 else jnp.concatenate(results, axis=1)
    return jnp.transpose(result, (2, 0, 1))


def solution(mesh):
    in_specs = (P("mod", "blk"), P())
    out_specs = P("mod", "blk", None)
    return jax.shard_map(body, mesh=mesh, in_specs=in_specs, out_specs=out_specs, check_vma=False)
```
